32 devices in a mesh: groups: 2 (over x), dp: 16 (over z, y, core).
Axes of the slice: x: 2, y: 2, z: 4, core: 2. Of those that a mesh axis runs over, the one named last changes fastest.
Arguments:
- inputs: bfloat16 [8192, 4096], P(('groups', 'dp')), parts along dimension 0, may hold values from -6 to 6
- gate_values: bfloat16 [8192, 4096], P(('groups', 'dp')), parts along dimension 0, may hold values from -6 to 6
- write_proj: bfloat16 [8192, 128], P(('groups', 'dp')), parts along dimension 0, may hold values from -6 to 6
- read_proj: bfloat16 [8192, 128], P(('groups', 'dp')), parts along dimension 0, may hold values from -0.59765625 to 0.59765625
- step_raw: bfloat16 [8192, 64], P(('groups', 'dp')), parts along dimension 0, may hold values from -3 to 10
- cotangent: bfloat16 [8192, 4096], P(('groups', 'dp')), parts along dimension 0, may hold values from -6 to 6
- step_bias: float32 [64], replicated, may hold values from -5.5 to -3.5
- rate_log: float32 [64], replicated
- skip_gain: float32 [64], replicated, may hold values from 0.5 to 1.5
- norm_gain: float32 [4096], replicated, may hold values from 0.5 to 1.5
- state_bank: bfloat16 [128, 64, 64, 128], P('groups', 'dp'), parts along dimension 0, may hold values from -1.796875 to 1.796875
- turn_index: int32 [8192], P(('groups', 'dp')), parts along dimension 0, may hold values from 0 to 3, as said below
- turn_slot: int32 [128], P('groups'), parts along dimension 0, may hold values from 0 to 63, each once
Outputs:
- grad_inputs: bfloat16 [8192, 4096], P(('groups', 'dp')), parts along dimension 0
- state_grad: bfloat16 [128, 64, 64, 128], P('groups', 'dp'), parts along dimension 0
- gain_grad: float32 [8192], P(('groups', 'dp')), parts along dimension 0
- head_grads: float32 [6, 64], P('groups'), parts along dimension 0
The draws below stay inside these ranges and needn't reach their ends.
There are 2 independent parts, one for each index of `groups`. The reference program is written for one: setup_inputs(seed, part) draws one part's arguments, and reference() takes and returns one part's arrays. A program takes and returns all parts, laid end to end along the dimension named above; an argument that names none is the same for every part. Nothing has to cross between parts.
Inputs may be any that keep to these rules, and one draw needn't show every extreme that they name: `turn_index`: within each device's 256 tokens turn numbers start at 0, never fall and rise by one at each new turn; some device has 4 turns. `turn_slot`: each slot number appears once.
All inputs are finite; a program needn't handle non-finite values.
Results may differ from the reference program's by a relative error of at most 0.0051.
Values may be sent and summed in bfloat16 or wider, within the bound.
No kernel may reach another device: no remote copies, remote signals or barrier semaphores. Data moves between devices by JAX's collectives and lax.ppermute only.
A program may use at most 128 MiB of HBM per device.

```python
import math
import jax
import jax.numpy as jnp
from jax import lax

LOCAL_HEADS = 64
HDIM = 64
DSTATE = 128
BLOCK_LEN = 256
DEVICE_ROWS = 256
TMAX = 4
TOTAL_TOKENS = 4096
SLOTS = 64
N_DP = 16


def draw_step_raw(key, part):
    jitter_key, spike_key = jax.random.split(key)
    block_list = TOTAL_TOKENS // DEVICE_ROWS
    jitter_values = jnp.clip(0.5 * jax.random.normal(jitter_key, (block_list, DEVICE_ROWS, LOCAL_HEADS), jnp.float32), -3.0, 3.0)
    spike_position = jax.random.randint(spike_key, (block_list, 2), 0, DEVICE_ROWS)
    token_positions = jnp.arange(DEVICE_ROWS, dtype=jnp.int32)
    spike_mask = jnp.any(token_positions[None, :, None] == spike_position[:, None, :], axis=2).astype(jnp.float32)
    return (jitter_values + 7.0 * spike_mask[:, :, None]).reshape(TOTAL_TOKENS, LOCAL_HEADS).astype(jnp.bfloat16)


def draw_rate_log(key, part):
    key_level = jax.random.fold_in(key, 0)
    levels = jax.random.uniform(key_level, (LOCAL_HEADS,), jnp.float32)
    low_end = math.log(20.0 / DEVICE_ROWS)
    return low_end + levels * (math.log(3.0) - low_end)


def draw_turn_index(key, part):
    block_list = TOTAL_TOKENS // DEVICE_ROWS
    stride = DEVICE_ROWS // TMAX
    key_cut, key_active, key_chosen = jax.random.split(key, 3)
    offsets = jax.random.randint(key_cut, (block_list, TMAX - 1), 0, stride - 1)
    cut_at = jnp.arange(TMAX - 1, dtype=jnp.int32)[None, :] * stride + 1 + offsets
    active = jax.random.randint(key_active, (block_list, TMAX - 1), 0, 2)
    chosen_block = jax.random.randint(key_chosen, (), 0, block_list)
    active = jnp.where(jnp.arange(block_list, dtype=jnp.int32)[:, None] == chosen_block, 1, active)
    token_positions = jnp.arange(DEVICE_ROWS, dtype=jnp.int32)
    turn_number = jnp.sum(active[:, None, :] * (token_positions[None, :, None] >= cut_at[:, None, :]).astype(jnp.int32), axis=2)
    return turn_number.reshape(TOTAL_TOKENS).astype(jnp.int32)


def strengthened(result, stream_key, source, target, parts, factor):
    owner, partner = [(jnp.arange(result.shape[axis_at]) // (result.shape[axis_at] // parts)).reshape([-1 if axis == axis_at else 1 for axis in range(result.ndim)]) for axis_at in (source, target)]
    chosen = jax.random.permutation(stream_key, parts)[partner]
    strong = (owner == chosen) | (owner == (partner + parts // 2) % parts)
    return jnp.where(strong, factor * result, result)


def block_levels(stream_key, shape, shards, smallest, high):
    loudness = 1.0
    for dim, shards_of in shards:
        heights = jax.random.uniform(jax.random.fold_in(jax.random.fold_in(stream_key, 6), dim), (shards_of,), jnp.float32, smallest / len(shards), high / len(shards))
        loudness = loudness * jnp.repeat(jnp.exp(heights), shape[dim] // shards_of).reshape((-1,) + (1,) * (len(shape) - 1 - dim))
    return loudness


def centred(rng, shape, scale, limit, cuts=(), held_as=jnp.bfloat16):
    level = block_levels(rng, shape, cuts, -0.22, 0.18) if cuts else 1.0
    drawn = jax.random.normal(rng, shape, jnp.float32) * scale * level
    return jnp.minimum(jnp.maximum(drawn, -limit), limit).astype(held_as)


def gaussian_with(rng, extent, deviation, reach, cuts, heavy, held_as=jnp.bfloat16):
    values = deviation * jax.random.normal(rng, extent, jnp.float32)
    if cuts:
        values = values * block_levels(rng, extent, cuts, -0.22, 0.18)
    return jnp.clip(strengthened(values, jax.random.fold_in(rng, 3), *heavy), -reach, reach).astype(held_as)


def setup_inputs(seed: int = 0, part: int = 0) -> dict:
    arg_keys = jax.random.split(jax.random.key(seed), 14)
    part_keys = jax.random.split(jax.random.fold_in(arg_keys[13], part), 14)
    return {
        "inputs": centred(part_keys[0], (TOTAL_TOKENS, LOCAL_HEADS * HDIM), 1.0, 6.0, ((0, 16),)),
        "gate_values": centred(part_keys[1], (TOTAL_TOKENS, LOCAL_HEADS * HDIM), 1.0, 6.0, ((0, 16),)),
        "write_proj": centred(part_keys[2], (TOTAL_TOKENS, DSTATE), 1.0, 6.0, ((0, 16),)),
        "read_proj": centred(part_keys[3], (TOTAL_TOKENS, DSTATE), 0.1, 0.59765625, ((0, 16),)),
        "step_raw": draw_step_raw(jax.random.fold_in(jax.random.fold_in(arg_keys[13], part), 71), part),
        "cotangent": gaussian_with(part_keys[5], (TOTAL_TOKENS, LOCAL_HEADS * HDIM), 1.0, 6.0, ((0, 16),), (0, 1, 16, 2.0)),
        "step_bias": jnp.clip(jax.random.uniform(arg_keys[6], (LOCAL_HEADS,), jnp.float32, -5.5, -3.5), -5.5, -3.5),
        "rate_log": draw_rate_log(jax.random.fold_in(arg_keys[13], 71), part),
        "skip_gain": jnp.clip(jax.random.uniform(arg_keys[8], (LOCAL_HEADS,), jnp.float32, 0.5, 1.5), 0.5, 1.5),
        "norm_gain": jnp.clip(1.0 + 0.1 * jax.random.normal(arg_keys[9], (LOCAL_HEADS * HDIM,), jnp.float32), 0.5, 1.5),
        "state_bank": centred(part_keys[10], (SLOTS, LOCAL_HEADS, HDIM, DSTATE), 0.3, 1.796875, ((1, 16),)),
        "turn_index": draw_turn_index(jax.random.fold_in(jax.random.fold_in(arg_keys[13], part), 71), part),
        "turn_slot": jax.random.permutation(part_keys[12], SLOTS).astype(jnp.int32),
    }


def project_turns(states, read_proj, turn_index):
    turn_cap = states.shape[0]
    onehot = turn_index[:, None] == jnp.arange(turn_cap, dtype=jnp.int32)[None, :]
    masked = jnp.where(onehot[:, :, None], read_proj.astype(jnp.float32)[:, None, :], jnp.zeros((), jnp.float32))
    return jnp.einsum('tgn,ghpn->thp', masked, states.astype(jnp.float32), precision=lax.Precision.HIGHEST).astype(jnp.bfloat16)

def turn_grads(read_grad, read_proj, turn_index, turn_cap):
    onehot = turn_index[:, None] == jnp.arange(turn_cap, dtype=jnp.int32)[None, :]
    masked = jnp.where(onehot[:, :, None], read_proj.astype(jnp.float32)[:, None, :], jnp.zeros((), jnp.float32))
    return jnp.einsum('tgn,thp->ghpn', masked, read_grad.astype(jnp.float32), precision=lax.Precision.HIGHEST)

def mixer(input_value, start_read, bias_value, rate_value, skip_value, gain_value, gate_values, write_proj, read_proj, step_raw, turn_index):
    row_count = input_value.shape[0]
    head_count = step_raw.shape[1]
    head_dim = input_value.shape[1] // head_count
    state_dim = write_proj.shape[1]
    block_count = row_count // BLOCK_LEN
    highest = lax.Precision.HIGHEST
    step_size = jax.nn.softplus(step_raw.astype(jnp.float32) + bias_value[None, :])
    log_decay = -jnp.exp(rate_value)[None, :] * step_size
    starts = jnp.concatenate([jnp.ones((1,), jnp.bool_), turn_index[1:] != turn_index[:-1]])
    blocked = (input_value.reshape(block_count, BLOCK_LEN, head_count, head_dim), write_proj.astype(jnp.float32).reshape(block_count, BLOCK_LEN, state_dim), read_proj.astype(jnp.float32).reshape(block_count, BLOCK_LEN, state_dim), step_size.reshape(block_count, BLOCK_LEN, head_count), log_decay.reshape(block_count, BLOCK_LEN, head_count), turn_index.reshape(block_count, BLOCK_LEN), starts.reshape(block_count, BLOCK_LEN), start_read.reshape(block_count, BLOCK_LEN, head_count, head_dim))
    token_positions = jnp.arange(BLOCK_LEN, dtype=jnp.int32)
    causal_mask = token_positions[:, None] >= token_positions[None, :]

    def advance(carried, pieces):
        state_now, since_now = carried
        block_x, block_write, block_read, block_step, block_decay, block_turn, block_start, block_begin = pieces
        running = jnp.cumsum(block_decay, axis=0)
        before = running - block_decay
        same_mask = (causal_mask & (block_turn[:, None] == block_turn[None, :]))[:, :, None]
        decay_mat = jnp.exp(jnp.where(same_mask, running[:, None, :] - running[None, :, :], -1e+30))
        offset = lax.optimization_barrier(jnp.max(jnp.where(same_mask, before[None, :, :], -1e+30), axis=1))
        scores = jnp.dot(block_read, block_write.T, precision=highest)
        weights = decay_mat * scores[:, :, None] * block_step[None, :, :]
        local_part = jnp.einsum('tsh,shp->thp', weights, block_x, precision=highest)
        kept = ((block_turn == block_turn[0]) & jnp.logical_not(block_start[0])).astype(jnp.float32)
        inner = running - offset
        projected = jnp.einsum('hpn,tn->thp', state_now, block_read, precision=highest)
        since = inner + kept[:, None] * since_now[None, :]
        carry_factor = jnp.exp(inner) * kept[:, None]
        output = local_part + carry_factor[:, :, None] * projected + jnp.exp(since)[:, :, None] * block_begin + skip_value[None, :, None] * block_x
        last_weights = decay_mat[-1] * block_step
        new_state = carry_factor[-1][:, None, None] * state_now + jnp.einsum('sh,shp,sn->hpn', last_weights, block_x, block_write, precision=highest)
        return ((new_state, since[-1]), output)
    start_state = (jnp.zeros((head_count, head_dim, state_dim), jnp.float32), jnp.zeros((head_count,), jnp.float32))
    final_state, outputs = lax.scan(advance, start_state, blocked)
    mixed = outputs.reshape(row_count, head_count, head_dim)
    gate_f = gate_values.astype(jnp.float32).reshape(row_count, head_count, head_dim)
    gated_out = mixed * jax.nn.silu(gate_f)
    mean_square = lax.optimization_barrier(jnp.mean(gated_out * gated_out, axis=-1, keepdims=True))
    normed = gated_out * lax.rsqrt(mean_square + 1e-05) * gain_value.reshape(head_count, head_dim)[None]
    return normed.reshape(row_count, head_count * head_dim)

def learner(inputs, start_read, step_bias, rate_log, skip_gain, norm_gain, gate_values, write_proj, read_proj, step_raw, turn_index, cotangent):

    def forward(input_value, read_value, bias_value, rate_value, skip_value, gain_value):
        return mixer(input_value, read_value, bias_value, rate_value, skip_value, gain_value, gate_values, write_proj, read_proj, step_raw, turn_index)
    primal, pullback = jax.vjp(forward, inputs.astype(jnp.float32), start_read.astype(jnp.float32), step_bias, rate_log, skip_gain, norm_gain)
    return pullback(cotangent.astype(jnp.float32))

def reference(inputs, gate_values, write_proj, read_proj, step_raw, cotangent, step_bias, rate_log, skip_gain, norm_gain, state_bank, turn_index, turn_slot):
    initial = state_bank[turn_slot].reshape(N_DP, TMAX, LOCAL_HEADS, HDIM, DSTATE)

    def split_rows(value):
        return value.reshape((N_DP, DEVICE_ROWS) + value.shape[1:])

    def per_block(pieces):
        start_read = project_turns(pieces[1], pieces[4], pieces[6])
        grads = learner(pieces[0], start_read, step_bias, rate_log, skip_gain, norm_gain, pieces[2], pieces[3], pieces[4], pieces[5], pieces[6], pieces[7])
        read_grad = grads[1].astype(jnp.bfloat16)
        state_part = turn_grads(read_grad, pieces[4], pieces[6], TMAX)
        return (grads[0], state_part, grads[2], grads[3], grads[4], grads[5])
    gradients = lax.map(per_block, (split_rows(inputs), initial, split_rows(gate_values), split_rows(write_proj), split_rows(read_proj), split_rows(step_raw), split_rows(turn_index), split_rows(cotangent)))
    grad_inputs = gradients[0].reshape(TOTAL_TOKENS, LOCAL_HEADS * HDIM).astype(jnp.bfloat16)
    flat_grads = gradients[1].reshape(N_DP * TMAX, LOCAL_HEADS, HDIM, DSTATE)
    state_grad = flat_grads[jnp.argsort(turn_slot)].astype(jnp.bfloat16)
    gain_grad = lax.optimization_barrier(jnp.sum(gradients[5], axis=0))
    head_grads = jnp.stack([lax.optimization_barrier(jnp.sum(gradients[2], axis=0)), lax.optimization_barrier(jnp.sum(gradients[3], axis=0)), lax.optimization_barrier(jnp.sum(gradients[4], axis=0))])
    return (grad_inputs, state_grad, gain_grad, head_grads)
```

```python
import functools

import jax
import jax.numpy as jnp
from jax import lax
from jax.experimental import pallas as pl
from jax.experimental.pallas import tpu as pltpu
from jax.sharding import PartitionSpec as P


TMAX = 4
EPS = 1e-5
LOG2E = 1.4426950408889634
F32 = jnp.float32
BF16 = jnp.bfloat16
HIGHEST = lax.Precision.HIGHEST
TURN_ROWS = 16


def nt_dot(a, b):
    return lax.dot_general(a, b, (((1,), (1,)), ((), ())), preferred_element_type=F32)


def nn_dot(a, b):
    return jnp.dot(a, b, preferred_element_type=F32)


def any_spec():
    return pl.BlockSpec(memory_space=pl.ANY)


def vmem_spec():
    return pl.BlockSpec(memory_space=pltpu.VMEM)


def smem_spec():
    return pl.BlockSpec(memory_space=pltpu.SMEM)


def bank_kernel(count, me_ref, slot_ref, bank_ref, out_ref, sem):
    me = me_ref[0]

    def copy(i):
        device = lax.bitwise_xor(me, 2 * (i // TMAX) + 1)
        slot = slot_ref[device * TMAX + i % TMAX]
        return pltpu.make_async_copy(bank_ref.at[slot], out_ref.at[i], sem.at[i])

    for i in range(count):
        copy(i).start()
    for i in range(count):
        copy(i).wait()


def pick_states(me, slots, bank):
    chips = slots.shape[0] // TMAX // 2
    count = chips * TMAX
    return pl.pallas_call(
        functools.partial(bank_kernel, count),
        out_shape=jax.ShapeDtypeStruct((count,) + bank.shape[1:], BF16),
        in_specs=[smem_spec(), smem_spec(), any_spec()],
        out_specs=vmem_spec(),
        scratch_shapes=[pltpu.SemaphoreType.DMA((count,))],
        cost_estimate=pl.CostEstimate(flops=0, transcendentals=0, bytes_accessed=4 * count * bank.shape[1] * bank.shape[2]),
        name="pick_states",
    )(me, slots, bank)


def turn_row(packed_ref, rows):
    pieces = [packed_ref[rows + i : rows + i + 1, :].astype(F32) for i in range(rows // 128)]
    return jnp.concatenate(pieces, axis=1)


def start_kernel(chips, width, rows, order, me_ref, slot_ref, bank_ref, lent_ref, *refs):
    packed = refs[:chips]
    outs = refs[chips : 2 * chips]
    all_ref, own, lent, sem, lent_sem, pack_sem = refs[2 * chips :]
    me = me_ref[0]
    core = lax.rem(me, 2)

    def pack_copy(j):
        return pltpu.make_async_copy(packed[j], all_ref.at[j], pack_sem.at[j])

    def copy(i):
        device = lax.bitwise_xor(me, 2 * (i // TMAX))
        slot = slot_ref[device * TMAX + i % TMAX]
        return pltpu.make_async_copy(bank_ref.at[slot], own.at[i], sem.at[i])

    def lent_copy(j):
        part = pl.ds(j * TMAX, TMAX)
        return pltpu.make_async_copy(lent_ref.at[part], lent.at[part], lent_sem.at[j])

    for j in order:
        pack_copy(j).start()
        for i in range(j * TMAX, (j + 1) * TMAX):
            copy(i).start()
        lent_copy(j).start()
    mine = pl.ds(pl.multiple_of(core * width, width), width)
    other = pl.ds(pl.multiple_of((1 - core) * width, width), width)
    for j in order:
        pack_copy(j).wait()
        proj = all_ref[j, :rows, :]
        turn = turn_row(all_ref.at[j], rows)
        for i in range(j * TMAX, (j + 1) * TMAX):
            copy(i).wait()
        lent_copy(j).wait()
        for source, place in ((own, mine), (lent, other)):
            total = jnp.zeros((width, rows), F32)
            for g in range(TMAX):
                part = nt_dot(source[j * TMAX + g], proj)
                total = jnp.where(turn == float(g), part, total)
            outs[j][place, :] = total.astype(BF16)


def start_reads(me, slots, bank, lent, packed, rows, order):
    chips = len(packed)
    width, state = bank.shape[1:]
    out_shape = [jax.ShapeDtypeStruct((2 * width, rows), BF16)] * chips
    out_shape.append(jax.ShapeDtypeStruct((chips,) + packed[0].shape, BF16))
    results = pl.pallas_call(
        functools.partial(start_kernel, chips, width, rows, order),
        out_shape=out_shape,
        in_specs=[smem_spec(), smem_spec()] + [any_spec()] * (chips + 2),
        out_specs=[vmem_spec()] * (chips + 1),
        scratch_shapes=[
            pltpu.VMEM((chips * TMAX, width, state), BF16),
            pltpu.VMEM((chips * TMAX, width, state), BF16),
            pltpu.SemaphoreType.DMA((chips * TMAX,)),
            pltpu.SemaphoreType.DMA((chips,)),
            pltpu.SemaphoreType.DMA((chips,)),
        ],
        cost_estimate=pl.CostEstimate(
            flops=2 * chips * TMAX * 2 * width * state * rows,
            transcendentals=0,
            bytes_accessed=chips * (TMAX * width * state * 4 + width * rows * 4),
        ),
        name="start_reads",
    )(me, slots, bank, lent, *packed)
    return results[:chips], results[chips]


def mix_kernel(
    chip_xor,
    heads,
    hdim,
    rows,
    me_ref,
    skip_ref,
    x_ref,
    gate_ref,
    cot_ref,
    inner_ref,
    source_ref,
    gain_ref,
    score_ref,
    begin_ref,
    *refs,
):
    same_ref, other_ref, grad_ref, stats_ref, gain_out_ref, high_ref, low_ref, begins, sem = refs[-9:]
    half = pl.program_id(0)
    width = heads * hdim
    device = lax.bitwise_xor(me_ref[0], 2 * chip_xor + half)
    fetch = pltpu.make_async_copy(begin_ref, begins, sem)

    @pl.when(half == 0)
    def _():
        fetch.start()

    mid = rows // 2
    x_t = x_ref[...].T
    gate_t = gate_ref[...].T
    cot_t = cot_ref[...].T
    gain_rows = jnp.broadcast_to(gain_ref[...], (8, width)).T
    inner = inner_ref[0]
    pad = jnp.zeros((8 - heads, rows), F32)
    source_cols = jnp.concatenate([source_ref[0], pad], axis=0).T

    @pl.when(half == 0)
    def _():
        fetch.wait()

    begin_rows = begins[pl.ds(pl.multiple_of(lax.rem(device, 2) * width, width), width), :]
    reads = []
    grads = []
    gains = []
    for h in range(heads):
        span = slice(h * hdim, (h + 1) * hdim)
        skip = skip_ref[device * heads + h]
        x_b = x_t[span]
        x = x_b.astype(F32)
        row = inner[h : h + 1, :]
        col = source_cols[:, h : h + 1]
        for low, high in ((0, 0), (0, 1), (1, 1)):
            source = slice(low * mid, (low + 1) * mid)
            target = slice(high * mid, (high + 1) * mid)
            weight = jnp.exp2(jnp.minimum(row[:, target] - col[source], 64.0)) * score_ref[source, target]
            rounded = weight.astype(BF16)
            high_ref[h, source, target] = rounded
            low_ref[source, target] = (weight - rounded.astype(F32)).astype(BF16)
        high_ref[h, mid:, :mid] = jnp.zeros((mid, mid), BF16)
        low_ref[mid:, :mid] = jnp.zeros((mid, mid), BF16)
        local = nn_dot(x_b, high_ref[h])
        grown = jnp.exp2(row)
        begin = grown * begin_rows[span].astype(F32)
        y = local + nn_dot(x_b, low_ref[...]) + begin + skip * x
        gate = gate_t[span].astype(F32)
        silu = gate / (1.0 + jnp.exp(-gate))
        gated = y * silu
        square = jnp.sum(gated * gated, axis=0, keepdims=True) * (1.0 / hdim)
        scale = lax.rsqrt(square + EPS)
        normed = gated * scale
        cot = cot_t[span].astype(F32)
        gains.append(cot * normed)
        dn = cot * gain_rows[span, 0:1]
        along = jnp.sum(dn * normed, axis=0, keepdims=True) * (1.0 / hdim)
        dy = (dn - normed * along) * scale * silu
        reads.append((grown * dy).astype(BF16))
        dy_b = dy.astype(BF16)
        d_x = nt_dot(dy_b, high_ref[h])
        grads.append((skip * dy + d_x).astype(BF16))
        taken = jnp.sum(x * d_x, axis=0, keepdims=True)
        given = jnp.sum(begin * dy + dy_b.astype(F32) * local, axis=0, keepdims=True)
        stats_ref[0, h, 0:1, :] = given - taken
        stats_ref[0, h, 1:2, :] = taken
        stats_ref[0, h, 2:3, :] = jnp.sum(x * dy, axis=0, keepdims=True)
        stats_ref[0, h, 3:8, :] = jnp.zeros((5, rows), F32)
    read = jnp.concatenate(reads, axis=0)

    @pl.when(half == 0)
    def _():
        same_ref[...] = read

    @pl.when(half == 1)
    def _():
        other_ref[...] = read

    grad_ref[...] = jnp.concatenate(grads, axis=0).T
    gain_part = jnp.concatenate(gains, axis=0)
    ones = jnp.ones((8, rows), BF16)
    gain_high = gain_part.astype(BF16)
    gain_low = (gain_part - gain_high.astype(F32)).astype(BF16)
    gain_out_ref[...] = nt_dot(ones, gain_high) + nt_dot(ones, gain_low)


def mix(me, chip_xor, skip, x, gate, cot, begin, inner, source, gain, score, previous, heads, hdim):
    rows, channels = x.shape
    width = heads * hdim
    devices = channels // width

    def device(half, me_ref):
        return lax.bitwise_xor(me_ref[0], 2 * chip_xor + half)

    columns = pl.BlockSpec((rows, width), lambda i, p: (0, device(i, p)))
    per_head = pl.BlockSpec((1, heads, rows), lambda i, p: (device(i, p), 0, 0))
    gain_spec = pl.BlockSpec((1, width), lambda i, p: (0, device(i, p)))
    whole = pl.BlockSpec((width, rows), lambda i, p: (0, 0))
    in_specs = [
        pl.BlockSpec(memory_space=pltpu.SMEM),
        columns,
        columns,
        columns,
        per_head,
        per_head,
        gain_spec,
        pl.BlockSpec((rows, rows), lambda i, p: (0, 0)),
        any_spec(),
    ]
    operands = [skip, x, gate, cot, inner, source, gain, score, begin]
    aliases = {}
    if previous is not None:
        for i, value in enumerate(previous):
            aliases[1 + len(operands)] = 2 + i
            operands.append(value)
            in_specs.append(any_spec())
    results = pl.pallas_call(
        functools.partial(mix_kernel, chip_xor, heads, hdim, rows),
        out_shape=[
            jax.ShapeDtypeStruct((width, rows), BF16),
            jax.ShapeDtypeStruct((width, rows), BF16),
            jax.ShapeDtypeStruct((rows, channels), BF16),
            jax.ShapeDtypeStruct((devices, heads, 8, rows), F32),
            jax.ShapeDtypeStruct((8, channels), F32),
        ],
        grid_spec=pltpu.PrefetchScalarGridSpec(
            num_scalar_prefetch=1,
            grid=(2,),
            in_specs=in_specs,
            out_specs=[
                whole,
                whole,
                columns,
                pl.BlockSpec((1, heads, 8, rows), lambda i, p: (device(i, p), 0, 0, 0)),
                pl.BlockSpec((8, width), lambda i, p: (0, device(i, p))),
            ],
            scratch_shapes=[
                pltpu.VMEM((heads, rows, rows), BF16),
                pltpu.VMEM((rows, rows), BF16),
                pltpu.VMEM((2 * width, rows), BF16),
                pltpu.SemaphoreType.DMA,
            ],
        ),
        input_output_aliases=aliases,
        cost_estimate=pl.CostEstimate(
            flops=12 * rows * rows * width,
            transcendentals=2 * heads * rows * rows,
            bytes_accessed=24 * rows * width,
        ),
        name="mix",
    )(me, *operands)
    return results[0], results[1], tuple(results[2:])


def state_kernel(partners, rows, me_ref, slot_ref, same_ref, other_ref, *refs):
    count = len(partners)
    reads = refs[:count]
    out_ref, buffer, held, packs, sem, read_sem, pack_sem = refs[-7:]
    me = me_ref[0]

    def copy(i, g):
        slot = slot_ref[lax.bitwise_xor(me, partners[i]) * TMAX + g]
        return pltpu.make_async_copy(buffer.at[i * TMAX + g], out_ref.at[slot], sem.at[i * TMAX + g])

    def read_copy(i):
        return pltpu.make_async_copy(reads[i], held.at[i], read_sem.at[i])

    def pack_copy(i):
        source = (other_ref if partners[i] % 2 else same_ref).at[partners[i] // 2]
        return pltpu.make_async_copy(source, packs.at[i], pack_sem.at[i])

    for i in range(count):
        read_copy(i).start()
        pack_copy(i).start()
    for i in range(count):
        read_copy(i).wait()
        pack_copy(i).wait()
        read = held[i].astype(F32)
        turn = turn_row(packs.at[i], rows)
        proj = packs[i, :rows, :]
        for g in range(TMAX):
            masked = jnp.where(turn == float(g), read, 0.0).astype(BF16)
            buffer[i * TMAX + g] = nn_dot(masked, proj).astype(BF16)
            copy(i, g).start()
    for i in range(count):
        for g in range(TMAX):
            copy(i, g).wait()


def state_grads(me, slots, partners, reads, packed_same, packed_other, previous, shape):
    width, rows = reads[0].shape
    count = len(partners)
    operands = [me, slots, packed_same, packed_other, *reads]
    in_specs = [smem_spec(), smem_spec()] + [any_spec()] * (count + 2)
    aliases = {}
    if previous is not None:
        aliases[len(operands)] = 0
        operands.append(previous)
        in_specs.append(any_spec())
    return pl.pallas_call(
        functools.partial(state_kernel, partners, rows),
        out_shape=jax.ShapeDtypeStruct(shape, BF16),
        in_specs=in_specs,
        out_specs=any_spec(),
        scratch_shapes=[
            pltpu.VMEM((count * TMAX,) + shape[1:], BF16),
            pltpu.VMEM((count, width, rows), BF16),
            pltpu.VMEM((count,) + packed_same.shape[1:], BF16),
            pltpu.SemaphoreType.DMA((count * TMAX,)),
            pltpu.SemaphoreType.DMA((count,)),
            pltpu.SemaphoreType.DMA((count,)),
        ],
        input_output_aliases=aliases,
        cost_estimate=pl.CostEstimate(
            flops=2 * count * TMAX * shape[1] * shape[2] * rows,
            transcendentals=0,
            bytes_accessed=count * (2 * TMAX * shape[1] * shape[2] + 4 * shape[1] * rows),
        ),
        name="state_grads",
    )(*operands)


def chip_order(chips):
    far = sorted(range(chips // 2, chips), key=lambda j: (j.bit_count(), j))
    return far + sorted(range(1, chips // 2), reverse=True)


def local(
    inputs,
    gate_values,
    write_proj,
    read_proj,
    step_raw,
    cotangent,
    step_bias,
    rate_log,
    skip_gain,
    norm_gain,
    state_bank,
    turn_index,
    turn_slot,
):
    devices = lax.axis_size("dp")
    chips = devices // 2
    slots, heads, hdim, dstate = state_bank.shape
    rows, _ = inputs.shape
    width = heads * hdim
    all_heads = devices * heads
    me = lax.axis_index("dp").astype(jnp.int32)
    me_array = me[None]

    def exchange(value, partner):
        return lax.ppermute(value, "dp", [(i, i ^ partner) for i in range(devices)])

    order = chip_order(chips)

    turn_values = turn_index.astype(BF16).reshape(rows // 128, 128)
    filler = jnp.zeros((TURN_ROWS - rows // 128, 128), BF16)
    packed_own = jnp.concatenate([read_proj, turn_values, filler], axis=0)
    packed = [packed_own] + [None] * (chips - 1)
    for j in order:
        packed[j] = exchange(packed_own, 2 * j)

    bank = state_bank.reshape(slots, width, dstate)
    lent = pick_states(me_array, turn_slot, bank)
    partner = exchange(lent, 1)
    begins, packed_all = start_reads(me_array, turn_slot, bank, partner, packed, rows, order + [0])
    packed_other = exchange(packed_all, 1)
    received = [begins[0]] + [None] * (chips - 1)
    for j in order:
        received[j] = exchange(begins[j], 2 * j)

    raw = step_raw.T.astype(F32) + step_bias[:, None]
    step = jax.nn.softplus(raw)
    pace = jnp.exp(rate_log)[:, None]
    rate = -pace * step
    position = jnp.arange(rows, dtype=jnp.int32)
    within = (position[:, None] <= position[None, :]) & (turn_index[:, None] == turn_index[None, :])
    within_f = within.astype(F32)
    inner = jnp.dot(rate, within_f, precision=HIGHEST)
    score = jnp.where(within, nt_dot(write_proj, read_proj), 0.0)
    inner_2 = inner * LOG2E
    inner_3 = inner_2.reshape(devices, heads, rows)
    source_3 = (inner_2 - jnp.log2(step)).reshape(devices, heads, rows)
    gain_row = norm_gain[None, :]

    previous = None
    back = {}
    for j in [0] + order:
        same, other, previous = mix(
            me_array,
            j,
            skip_gain,
            inputs,
            gate_values,
            cotangent,
            received[j],
            inner_3,
            source_3,
            gain_row,
            score,
            previous,
            heads,
            hdim,
        )
        back[2 * j] = same if j == 0 else exchange(same, 2 * j)
        back[2 * j + 1] = exchange(other, 2 * j + 1)
    grad_inputs, stats, gain_part = previous

    stats = stats.reshape(all_heads, 8, rows)
    d_rate = jnp.dot(stats[:, 0], within_f.T, precision=HIGHEST)
    d_step = stats[:, 1] / step - pace * d_rate
    head_part = jnp.stack(
        [
            jnp.sum(d_step * jax.nn.sigmoid(raw), axis=1),
            jnp.sum(d_rate * rate, axis=1),
            jnp.sum(stats[:, 2], axis=1),
        ]
    )
    gain_lines = gain_part[0].reshape(devices, width // 128, 128)
    head_count = 3 * all_heads
    head_lines = -(-head_count // 128)
    head_flat = jnp.pad(head_part.reshape(head_count), (0, head_lines * 128 - head_count))
    head_block = jnp.broadcast_to(head_flat.reshape(1, head_lines, 128), (devices, head_lines, 128))
    rest = jnp.zeros((devices, 8 - head_lines - width // 128, 128), F32)
    small = jnp.concatenate([gain_lines, head_block, rest], axis=1)
    small = jnp.sum(lax.all_to_all(small, "dp", split_axis=0, concat_axis=0, tiled=True), axis=0)
    gain_grad = small[: width // 128].reshape(width)
    head_grads = small[width // 128 : width // 128 + head_lines].reshape(-1)[:head_count].reshape(3, all_heads)

    sequence = [0, 1]
    for j in order:
        sequence += [2 * j, 2 * j + 1]
    cut = len(sequence) // 2
    state = None
    for part in (sequence[:cut], sequence[cut:]):
        state = state_grads(
            me_array,
            turn_slot,
            part,
            [back[q] for q in part],
            packed_all,
            packed_other,
            state,
            (slots, width, dstate),
        )
    return (grad_inputs, state.reshape(state_bank.shape), gain_grad, head_grads)


def solution(mesh):
    in_specs = (
        P(("groups", "dp"), None),
        P(("groups", "dp"), None),
        P(("groups", "dp"), None),
        P(("groups", "dp"), None),
        P(("groups", "dp"), None),
        P(("groups", "dp"), None),
        P(),
        P(),
        P(),
        P(),
        P("groups", "dp", None, None),
        P(("groups", "dp")),
        P("groups"),
    )
    out_specs = (
        P(("groups", "dp"), None),
        P("groups", "dp", None, None),
        P(("groups", "dp")),
        P("groups", None),
    )

    return jax.shard_map(local, mesh=mesh, in_specs=in_specs, out_specs=out_specs, check_vma=False)
```
